32 devices in a mesh: band: 8 (over z, core), slab: 4 (over y, x).
Axes of the slice: x: 2, y: 2, z: 4, core: 2. Of those that a mesh axis runs over, the one named last changes fastest.
Arguments:
- orbitals: float32 [9216, 24, 256], P('band', 'slab'), may hold values from -6 to 6
- rotation: float32 [9216, 512], P('band'), may hold values from -0.09375 to 0.09375
- occupation: float32 [512], P('band'), may hold values from 0.2 to 2, as said below
- metric: float32 [3, 3], replicated, may hold values from -0.3 to 1.4, as said below
Outputs:
- rotated_orbitals: float32 [512, 24, 256], P('band', 'slab')
- density: float32 [24, 16], P('slab')
The draws below stay inside these ranges and needn't reach their ends.
Inputs may be any that keep to these rules, and one draw needn't show every extreme that they name: `occupation`: positive occupations. `metric`: symmetric with a dominant positive diagonal.
All inputs are finite; a program needn't handle non-finite values.
Results may differ from the reference program's by a relative error of at most 0.000071.
Values sent between devices are 32-bit elements; how exact they have to be, the bound alone decides.
A program may use at most 64 MiB of HBM per device.

```python
import jax
import jax.numpy as jnp
from jax import lax

NORB = 9216
PANEL = 256
PANELS = 2
WIN = 512
PY = 4
PX = 4
PLANE = 256
NZ = 24


def draw_occupation(key, part):
    window = PANEL * PANELS
    position = jnp.arange(window, dtype=jnp.float32) / (window - 1)
    factor = jnp.clip(1.0 + 0.2 * jax.random.normal(key, (window,), jnp.float32), 0.5, 1.5)
    return jnp.exp(jnp.log(3.0) * position) * factor / 2.25


def draw_metric(key, part):
    first_key = jax.random.fold_in(key, 11)
    second_key = jax.random.fold_in(key, 12)
    diagonal = jax.random.uniform(first_key, (3,), jnp.float32, 0.7, 1.4)
    offdiag = jax.random.uniform(second_key, (3,), jnp.float32, -0.25, 0.25)
    matrix = jnp.diag(diagonal)
    matrix = matrix.at[0, 1].set(offdiag[0]).at[1, 0].set(offdiag[0])
    matrix = matrix.at[0, 2].set(offdiag[1]).at[2, 0].set(offdiag[1])
    matrix = matrix.at[1, 2].set(offdiag[2]).at[2, 1].set(offdiag[2])
    return matrix


def strengthened(array, stream_key, source, target, blocks, factor):
    owner, partner = [(jnp.arange(array.shape[axis_at]) // (array.shape[axis_at] // blocks)).reshape([-1 if axis == axis_at else 1 for axis in range(array.ndim)]) for axis_at in (source, target)]
    chosen = jax.random.permutation(stream_key, blocks)[partner]
    strong = (owner == chosen) | (owner == (partner + blocks // 2) % blocks)
    return jnp.where(strong, factor * array, array)


def level_of(rng, extent, split, low, largest):
    level = 1.0
    for dim, shards_of in split:
        draws = jax.random.uniform(jax.random.fold_in(jax.random.fold_in(rng, 6), dim), (shards_of,), jnp.float32, low / len(split), largest / len(split))
        level = level * jnp.repeat(jnp.exp(draws), extent[dim] // shards_of).reshape((-1,) + (1,) * (len(extent) - 1 - dim))
    return level


def centred(own_key, dims, scale, bound, cuts=(), held_as=jnp.bfloat16):
    gain = level_of(own_key, dims, cuts, -0.22, 0.18) if cuts else 1.0
    array = jax.random.normal(own_key, dims, jnp.float32) * scale * gain
    return jnp.minimum(jnp.maximum(array, -bound), bound).astype(held_as)


def bell_draw_with(own_key, shape, width, most, split, heavy, held_as=jnp.bfloat16):
    entries = width * jax.random.normal(own_key, shape, jnp.float32)
    if split:
        entries = entries * level_of(own_key, shape, split, -0.22, 0.18)
    return jnp.clip(strengthened(entries, jax.random.fold_in(own_key, 3), *heavy), -most, most).astype(held_as)


def setup_inputs(seed: int = 0) -> dict:
    streams_of = jax.random.split(jax.random.key(seed), 5)
    return {
        "orbitals": centred(streams_of[0], (NORB, NZ, PLANE), 1.0, 6.0, ((0, 8), (1, 4)), jnp.float32),
        "rotation": bell_draw_with(streams_of[1], (NORB, WIN), NORB ** -0.5, 0.09375, ((0, 8),), (0, 1, 8, 2.0), jnp.float32),
        "occupation": draw_occupation(jax.random.fold_in(streams_of[4], 71), 0),
        "metric": draw_metric(jax.random.fold_in(streams_of[4], 71), 0),
    }


STENCIL_WEIGHTS = (6.0 / 7.0, -15.0 / 56.0, 5.0 / 63.0, -1.0 / 56.0, 6.0 / 1925.0, -1.0 / 5544.0)


def inner_derivative(field, axis_number, count):
    summed = jnp.zeros_like(lax.slice_in_dim(field, 6, 6 + count, axis=axis_number))
    for distance, weight in enumerate(STENCIL_WEIGHTS, start=1):
        ahead = lax.slice_in_dim(field, 6 + distance, 6 + distance + count, axis=axis_number)
        behind = lax.slice_in_dim(field, 6 - distance, 6 - distance + count, axis=axis_number)
        summed = summed + weight * (ahead - behind)
    return summed


def periodic_derivative(field, axis_number):
    summed = jnp.zeros_like(field)
    for distance, weight in enumerate(STENCIL_WEIGHTS, start=1):
        summed = summed + weight * (jnp.roll(field, -distance, axis_number) - jnp.roll(field, distance, axis_number))
    return summed


def reference(orbitals, rotation, occupation, metric):
    window = PANEL * PANELS
    stored_y = PY + 12
    stored_x = PX + 12
    rotated = lax.dot_general(rotation, orbitals.reshape(NORB, NZ * PLANE), (((0,), (0,)), ((), ())), precision=lax.Precision.HIGHEST, preferred_element_type=jnp.float32)
    fields = rotated.reshape(window, NZ, stored_y, stored_x)
    row_band = fields[:, :, 6:6 + PY, :]
    column_band = fields[:, :, :, 6:6 + PX]
    interior = fields[:, :, 6:6 + PY, 6:6 + PX]
    components = (inner_derivative(row_band, 3, PX), inner_derivative(column_band, 2, PY), periodic_derivative(interior, 1))
    quadratic = jnp.zeros_like(interior)
    for left_axis in range(3):
        for right_axis in range(3):
            quadratic = quadratic + metric[left_axis, right_axis] * components[left_axis] * components[right_axis]
    density = jnp.einsum("w,wc->c", occupation, quadratic.reshape(window, NZ * PY * PX), precision=lax.Precision.HIGHEST)
    density = density * (0.5 / window)
    return rotated.reshape(window, NZ, PLANE), density.reshape(NZ, PY * PX)
```

```python
import functools

import jax
import jax.numpy as jnp
import numpy as np
from jax import lax
from jax.experimental import pallas as pl
from jax.experimental.pallas import tpu as pltpu
from jax.sharding import PartitionSpec as P

PY = 4
PX = 4
LANES = 128
REACH = 6
MESH = pl.DeviceIdType.MESH
STENCIL_WEIGHTS = (6.0 / 7.0, -15.0 / 56.0, 5.0 / 63.0, -1.0 / 56.0, 6.0 / 1925.0, -1.0 / 5544.0)
HIGHEST = lax.Precision.HIGHEST


def plane_tables():
    stored_x = PX + 12
    table = np.zeros(((PY + 12) * stored_x, 3 * LANES), np.float32)
    for row_y in range(PY):
        for row_x in range(PX):
            point = row_y * PX + row_x
            centre = (row_y + 6) * stored_x + row_x + 6
            table[centre, point] = 1.0
            for distance, weight in enumerate(STENCIL_WEIGHTS, start=1):
                table[centre + distance, LANES + point] += weight
                table[centre - distance, LANES + point] -= weight
                table[centre + distance * stored_x, 2 * LANES + point] += weight
                table[centre - distance * stored_x, 2 * LANES + point] -= weight
    return table


def depth_tables(planes, hops):
    points = PY * PX
    table = np.zeros((2 * hops + 1, LANES, LANES), np.float32)
    for plane in range(planes):
        for distance, weight in enumerate(STENCIL_WEIGHTS, start=1):
            for signed, value in ((distance, weight), (-distance, -weight)):
                slab, source = divmod(plane + signed, planes)
                for point in range(points):
                    table[slab + hops, source * points + point, plane * points + point] += value
    return table


def kernel(
    sizes, orb_hbm, rot_hbm, occ_ref, metric_ref, plane_ref, depth_ref, out_ref, dens_ref,
    orb, rot, left, part, crecv, sbuf, line, halo, terms,
    orb_sem, rot_sem, core_send, core_recv, line_send, line_recv, halo_send, halo_recv, term_send, term_recv,
):
    bands, slabs, planes, owned, hops, window = sizes
    chips = bands // 2
    me, slab = lax.axis_index("band"), lax.axis_index("slab")
    chip, core = me // 2, me % 2
    partner = (chip * 2 + 1 - core, slab)
    ahead, behind = (me + 2, slab), (me - 2, slab)

    def load(p):
        return pltpu.make_async_copy(orb_hbm.at[p], orb.at[p], orb_sem.at[p])

    load_rot = pltpu.make_async_copy(rot_hbm, rot, rot_sem)
    load_rot.start()
    for p in range(planes):
        load(p).start()

    barrier = pltpu.get_barrier_semaphore()
    for k in range(1, bands):
        pl.semaphore_signal(barrier, inc=1, device_id=((me + k) % bands, slab), device_id_type=MESH)
    offsets = [h for h in range(-hops, hops + 1) if h != 0]
    for h in offsets:
        pl.semaphore_signal(barrier, inc=1, device_id=(me, (slab + h + slabs) % slabs), device_id_type=MESH)

    load_rot.wait()
    for chip_at in range(chips):
        rows = jnp.transpose(rot[:, chip_at * 2 * owned : (chip_at + 1) * 2 * owned])
        high = rows.astype(jnp.bfloat16)
        low = (rows - high.astype(jnp.float32)).astype(jnp.bfloat16)
        for core_at in range(2):
            at = (core_at * chips + chip_at) * owned
            left[at : at + owned, :] = high[core_at * owned : (core_at + 1) * owned]
            left[window + at : window + at + owned, :] = low[core_at * owned : (core_at + 1) * owned]

    def core_copy(p):
        return pltpu.make_async_remote_copy(
            src_ref=part.at[p, 1 - core], dst_ref=crecv.at[p], send_sem=core_send.at[p], recv_sem=core_recv.at[p],
            device_id=partner, device_id_type=MESH,
        )

    def multiply(p):
        load(p).wait()
        field = orb[p]
        high = field.astype(jnp.bfloat16)
        low = (field - high.astype(jnp.float32)).astype(jnp.bfloat16)
        both = jnp.dot(left[...], high, preferred_element_type=jnp.float32)
        small = jnp.dot(left[:window, :], low, preferred_element_type=jnp.float32)
        total = both[:window] + (both[window:] + small)
        part[p] = total.reshape(2, window // 2, total.shape[-1])

    def line_copy(direction, p, t, src, target):
        return pltpu.make_async_remote_copy(
            src_ref=src, dst_ref=line.at[direction, p, t],
            send_sem=line_send.at[direction, p, t], recv_sem=line_recv.at[direction, p, t],
            device_id=target, device_id_type=MESH,
        )

    def block(d):
        return pl.ds(pl.multiple_of(d * owned, owned), owned)

    def originate(p):
        core_copy(p).wait_recv()
        sbuf[p] = part[p, core] + crecv[p]
        for t in range(chips - 1):
            @pl.when(chip == 0)
            def _():
                line_copy(0, p, t, sbuf.at[p, block(chips - 1 - t)], ahead).start()

            @pl.when(chip == chips - 1)
            def _():
                line_copy(1, p, t, sbuf.at[p, block(t)], behind).start()
        out_ref[p] = sbuf[p, block(chip), :]

    def forward(p):
        def rightward(t):
            @pl.when((chip > 0) & (chip < chips - 1 - t))
            def _():
                line_copy(0, p, t, line.at[0, p, t], behind).wait_recv()
                line[0, p, t] += sbuf[p, block(chips - 1 - t), :]
                line_copy(0, p, t, line.at[0, p, t], ahead).start()

        def leftward(t):
            @pl.when((chip < chips - 1) & (chip > t))
            def _():
                line_copy(1, p, t, line.at[1, p, t], ahead).wait_recv()
                line[1, p, t] += sbuf[p, block(t), :]
                line_copy(1, p, t, line.at[1, p, t], behind).start()

        @pl.when(chip < chips // 2)
        def _():
            for t in range(chips - 1):
                rightward(t)
            for t in range(chips - 1):
                leftward(t)

        @pl.when(chip >= chips // 2)
        def _():
            for t in range(chips - 1):
                leftward(t)
            for t in range(chips - 1):
                rightward(t)

        @pl.when(chip > 0)
        def _():
            t = chips - 1 - chip
            line_copy(0, p, t, line.at[0, p, t], behind).wait_recv()
            out_ref[p] += line[0, p, t]

        @pl.when(chip < chips - 1)
        def _():
            line_copy(1, p, chip, line.at[1, p, chip], ahead).wait_recv()
            out_ref[p] += line[1, p, chip]

    multiply(0)
    pl.semaphore_wait(barrier, bands - 1 + len(offsets))
    core_copy(0).start()

    def step(p, carry):
        multiply(p)
        core_copy(p).start()
        originate(p - 1)
        return carry

    lax.fori_loop(1, planes, step, 0)
    originate(planes - 1)

    def onward(p, carry):
        forward(p)
        return carry

    lax.fori_loop(0, planes, onward, 0)

    points = PY * PX
    table = plane_ref[...]
    values = jnp.zeros((owned, 3 * LANES), jnp.float32)
    for p in range(planes):
        part_values = jnp.dot(out_ref[p], table, precision=HIGHEST, preferred_element_type=jnp.float32)
        if p:
            part_values = jnp.concatenate(
                [pltpu.roll(part_values[:, g * LANES : (g + 1) * LANES], p * points, 1) for g in range(3)], axis=1
            )
        values = values + part_values
    halo[hops] = values[:, :LANES]
    grad_x = values[:, LANES : 2 * LANES]
    grad_y = values[:, 2 * LANES :]

    def halo_copy(number, h):
        return pltpu.make_async_remote_copy(
            src_ref=halo.at[hops], dst_ref=halo.at[hops - h],
            send_sem=halo_send.at[number], recv_sem=halo_recv.at[number],
            device_id=(me, (slab + h + slabs) % slabs), device_id_type=MESH,
        )

    copies = [halo_copy(number, h) for number, h in enumerate(offsets)]
    for copy in copies:
        copy.start()
    grad_z = jnp.dot(halo[hops], depth_ref[hops], precision=HIGHEST, preferred_element_type=jnp.float32)
    for copy, h in zip(copies, offsets):
        copy.wait()
        grad_z = grad_z + jnp.dot(
            halo[hops - h], depth_ref[hops - h], precision=HIGHEST, preferred_element_type=jnp.float32
        )
    components = (grad_x, grad_y, grad_z)
    quadratic = jnp.zeros_like(grad_x)
    for i in range(3):
        for j in range(3):
            quadratic = quadratic + metric_ref[i, j] * components[i] * components[j]
    term = jnp.dot(occ_ref[...], quadratic, precision=HIGHEST, preferred_element_type=jnp.float32)
    terms[me] = jnp.broadcast_to(term, (8, LANES))

    def term_copy(k):
        return pltpu.make_async_remote_copy(
            src_ref=terms.at[me], dst_ref=terms.at[me],
            send_sem=term_send.at[k - 1], recv_sem=term_recv.at[k - 1],
            device_id=((me + k) % bands, slab), device_id_type=MESH,
        )

    for k in range(1, bands):
        term_copy(k).start()

    def sent(p, carry):
        core_copy(p).wait_send()
        for t in range(chips - 1):
            @pl.when(chip < chips - 1 - t)
            def _():
                line_copy(0, p, t, line.at[0, p, t], ahead).wait_send()

            @pl.when(chip > t)
            def _():
                line_copy(1, p, t, line.at[1, p, t], behind).wait_send()
        return carry

    lax.fori_loop(0, planes, sent, 0)
    for k in range(1, bands):
        term_copy(k).wait()
    summed = terms[0]
    for b in range(1, bands):
        summed = summed + terms[b]
    summed = summed * (0.5 / window)
    for p in range(planes):
        dens_ref[p : p + 1, :] = summed[0:1, p * points : (p + 1) * points]


def local(orbitals, rotation, occupation, metric):
    bands, slabs = lax.axis_size("band"), lax.axis_size("slab")
    orbital_count, planes, plane_size = orbitals.shape
    window = rotation.shape[1]
    owned = window // bands
    chips = bands // 2
    hops = -(-REACH // planes)
    f32 = jnp.float32
    vmem = pl.BlockSpec(memory_space=pltpu.VMEM)
    hbm = pl.BlockSpec(memory_space=pl.ANY)
    dma = pltpu.SemaphoreType.DMA
    neighbours = 2 * hops
    rotated, density = pl.pallas_call(
        functools.partial(kernel, (bands, slabs, planes, owned, hops, window)),
        out_shape=(
            jax.ShapeDtypeStruct((planes, owned, plane_size), f32),
            jax.ShapeDtypeStruct((planes, PY * PX), f32),
        ),
        in_specs=[hbm, hbm, vmem, pl.BlockSpec(memory_space=pltpu.SMEM), vmem, vmem],
        out_specs=(vmem, vmem),
        scratch_shapes=[
            pltpu.VMEM((planes, orbital_count, plane_size), f32),
            pltpu.VMEM((orbital_count, window), f32),
            pltpu.VMEM((2 * window, orbital_count), jnp.bfloat16),
            pltpu.VMEM((planes, 2, window // 2, plane_size), f32),
            pltpu.VMEM((planes, window // 2, plane_size), f32),
            pltpu.VMEM((planes, window // 2, plane_size), f32),
            pltpu.VMEM((2, planes, chips - 1, owned, plane_size), f32),
            pltpu.VMEM((neighbours + 1, owned, LANES), f32),
            pltpu.VMEM((bands, 8, LANES), f32),
            dma((planes,)),
            dma,
            dma((planes,)),
            dma((planes,)),
            dma((2, planes, chips - 1)),
            dma((2, planes, chips - 1)),
            dma((neighbours,)),
            dma((neighbours,)),
            dma((bands - 1,)),
            dma((bands - 1,)),
        ],
        compiler_params=pltpu.CompilerParams(
            collective_id=0, has_side_effects=True, vmem_limit_bytes=48 * 1024 * 1024
        ),
    )(
        jnp.transpose(orbitals, (1, 0, 2)),
        rotation,
        occupation.reshape(1, owned),
        metric,
        jnp.asarray(plane_tables()),
        jnp.asarray(depth_tables(planes, hops)),
    )
    return jnp.transpose(rotated, (1, 0, 2)), density


def solution(mesh):
    placed = (P("band", "slab", None), P("band", None), P("band"), P())
    return jax.shard_map(
        local,
        mesh=mesh,
        in_specs=placed,
        out_specs=(P("band", "slab", None), P("slab", None)),
        check_vma=False,
    )
```

```python
import functools

import jax
import jax.numpy as jnp
import ml_dtypes
import numpy as np
from jax import lax
from jax.experimental import pallas as pl
from jax.experimental.pallas import tpu as pltpu
from jax.sharding import PartitionSpec as P

PY = 4
PX = 4
LANES = 128
REACH = 6
MESH = pl.DeviceIdType.MESH
STENCIL_WEIGHTS = (6.0 / 7.0, -15.0 / 56.0, 5.0 / 63.0, -1.0 / 56.0, 6.0 / 1925.0, -1.0 / 5544.0)
HIGHEST = lax.Precision.HIGHEST


def plane_tables():
    stored_x = PX + 12
    table = np.zeros(((PY + 12) * stored_x, 3 * LANES), np.float32)
    for row_y in range(PY):
        for row_x in range(PX):
            point = row_y * PX + row_x
            centre = (row_y + 6) * stored_x + row_x + 6
            table[centre, point] = 1.0
            for distance, weight in enumerate(STENCIL_WEIGHTS, start=1):
                table[centre + distance, LANES + point] += weight
                table[centre - distance, LANES + point] -= weight
                table[centre + distance * stored_x, 2 * LANES + point] += weight
                table[centre - distance * stored_x, 2 * LANES + point] -= weight
    return table


def depth_tables(planes, hops):
    points = PY * PX
    table = np.zeros((2 * hops + 1, LANES, LANES), np.float32)
    for plane in range(planes):
        for distance, weight in enumerate(STENCIL_WEIGHTS, start=1):
            for signed, value in ((distance, weight), (-distance, -weight)):
                slab, source = divmod(plane + signed, planes)
                for point in range(points):
                    table[slab + hops, source * points + point, plane * points + point] += value
    return table


def split_dot(x, table):
    depth = x.shape[1]
    high = x.astype(jnp.bfloat16)
    low = (x - high.astype(jnp.float32)).astype(jnp.bfloat16)
    f32 = jnp.float32
    main = jnp.dot(high, table[:depth], preferred_element_type=f32)
    rest = jnp.dot(low, table[:depth], preferred_element_type=f32)
    return main + (rest + jnp.dot(high, table[depth:], preferred_element_type=f32))


def halves(table):
    high = table.astype(ml_dtypes.bfloat16)
    low = (table - high.astype(np.float32)).astype(ml_dtypes.bfloat16)
    return jnp.asarray(np.concatenate([high, low], axis=0))


def kernel(
    sizes, orb_hbm, rot_hbm, occ_hbm, metric_hbm, plane_hbm, depth_hbm, out_ref, dens_ref,
    occ_ref, metric_ref, plane_ref, depth_ref, values, small_sem, orb, rot, left, part, crecv, sbuf, line, halo, terms,
    orb_sem, rot_sem, core_send, core_recv, line_send, line_recv, halo_send, halo_recv, term_send, term_recv,
):
    bands, slabs, planes, owned, hops, window = sizes
    chips = bands // 2
    me, slab = lax.axis_index("band"), lax.axis_index("slab")
    chip, core = me // 2, me % 2
    points = PY * PX
    partner = (chip * 2 + 1 - core, slab)
    ahead, behind = (me + 2, slab), (me - 2, slab)

    def load(p):
        return pltpu.make_async_copy(orb_hbm.at[p], orb.at[p], orb_sem.at[p])

    load_rot = pltpu.make_async_copy(rot_hbm, rot, rot_sem)
    load_rot.start()
    for p in range(planes):
        load(p).start()
    small_loads = [
        pltpu.make_async_copy(src, dst, small_sem.at[n])
        for n, (src, dst) in enumerate(
            ((occ_hbm, occ_ref), (metric_hbm, metric_ref), (plane_hbm, plane_ref), (depth_hbm, depth_ref))
        )
    ]
    for small_load in small_loads:
        small_load.start()

    barrier = pltpu.get_barrier_semaphore()
    for k in range(1, bands):
        pl.semaphore_signal(barrier, inc=1, device_id=((me + k) % bands, slab), device_id_type=MESH)
    offsets = [h for h in range(-hops, hops + 1) if h != 0]
    for h in offsets:
        pl.semaphore_signal(barrier, inc=1, device_id=(me, (slab + h + slabs) % slabs), device_id_type=MESH)

    load_rot.wait()
    for chip_at in range(chips):
        rows = jnp.transpose(rot[:, chip_at * 2 * owned : (chip_at + 1) * 2 * owned])
        high = rows.astype(jnp.bfloat16)
        low = (rows - high.astype(jnp.float32)).astype(jnp.bfloat16)
        for core_at in range(2):
            at = (core_at * chips + chip_at) * owned
            left[at : at + owned, :] = high[core_at * owned : (core_at + 1) * owned]
            left[window + at : window + at + owned, :] = low[core_at * owned : (core_at + 1) * owned]

    def core_copy(p):
        return pltpu.make_async_remote_copy(
            src_ref=part.at[p, 1 - core], dst_ref=crecv.at[p], send_sem=core_send.at[p], recv_sem=core_recv.at[p],
            device_id=partner, device_id_type=MESH,
        )

    def multiply(p):
        load(p).wait()
        field = orb[p]
        high = field.astype(jnp.bfloat16)
        low = (field - high.astype(jnp.float32)).astype(jnp.bfloat16)
        both = jnp.dot(left[...], high, preferred_element_type=jnp.float32)
        small = jnp.dot(left[:window, :], low, preferred_element_type=jnp.float32)
        total = both[:window] + (both[window:] + small)
        part[p] = total.reshape(2, window // 2, total.shape[-1])

    def line_copy(direction, p, t, src, target):
        return pltpu.make_async_remote_copy(
            src_ref=src, dst_ref=line.at[direction, p, t],
            send_sem=line_send.at[direction, p, t], recv_sem=line_recv.at[direction, p, t],
            device_id=target, device_id_type=MESH,
        )

    def block(d):
        return pl.ds(pl.multiple_of(d * owned, owned), owned)

    def originate(p):
        core_copy(p).wait_recv()
        sbuf[p] = part[p, core] + crecv[p]
        for t in range(chips - 1):
            @pl.when(chip == 0)
            def _():
                @pl.when(p > 0)
                def _():
                    line_copy(0, p - 1, t, sbuf.at[p - 1, block(chips - 1 - t)], ahead).wait_send()

                line_copy(0, p, t, sbuf.at[p, block(chips - 1 - t)], ahead).start()

            @pl.when(chip == chips - 1)
            def _():
                @pl.when(p > 0)
                def _():
                    line_copy(1, p - 1, t, sbuf.at[p - 1, block(t)], behind).wait_send()

                line_copy(1, p, t, sbuf.at[p, block(t)], behind).start()
        out_ref[p] = sbuf[p, block(chip), :]

    def transit(p):
        def rightward(t):
            @pl.when((chip > 0) & (chip < chips - 1 - t))
            def _():
                line_copy(0, p, t, line.at[0, p, t], behind).wait_recv()
                line[0, p, t] += sbuf[p, block(chips - 1 - t), :]
                line_copy(0, p, t, line.at[0, p, t], ahead).start()

        def leftward(t):
            @pl.when((chip < chips - 1) & (chip > t))
            def _():
                line_copy(1, p, t, line.at[1, p, t], ahead).wait_recv()
                line[1, p, t] += sbuf[p, block(t), :]
                line_copy(1, p, t, line.at[1, p, t], behind).start()

        @pl.when(chip < chips // 2)
        def _():
            for t in range(chips - 1):
                rightward(t)
            for t in range(chips - 1):
                leftward(t)

        @pl.when(chip >= chips // 2)
        def _():
            for t in range(chips - 1):
                leftward(t)
            for t in range(chips - 1):
                rightward(t)

    def finish(p):
        @pl.when(chip > 0)
        def _():
            t = chips - 1 - chip
            line_copy(0, p, t, line.at[0, p, t], behind).wait_recv()
            out_ref[p] += line[0, p, t]

        @pl.when(chip < chips - 1)
        def _():
            line_copy(1, p, chip, line.at[1, p, chip], ahead).wait_recv()
            out_ref[p] += line[1, p, chip]

        found = split_dot(out_ref[p], plane_ref[...])
        for g in range(3):
            group = found[:, g * LANES : (g + 1) * LANES]
            values[:, g * LANES : (g + 1) * LANES] += pltpu.roll(group, p * points, 1)

    multiply(0)
    pl.semaphore_wait(barrier, bands - 1 + len(offsets))
    core_copy(0).start()
    values[...] = jnp.zeros_like(values)
    for small_load in small_loads:
        small_load.wait()

    def step(p, carry):
        multiply(p)
        core_copy(p).start()
        originate(p - 1)

        @pl.when(p >= 2)
        def _():
            transit(p - 2)

        @pl.when(p >= 3)
        def _():
            finish(p - 3)

        return carry

    lax.fori_loop(1, planes, step, 0)
    originate(planes - 1)

    def drain(p, carry):
        transit(p)
        finish(p - 1)
        return carry

    transit(planes - 2)
    finish(planes - 3)
    lax.fori_loop(planes - 1, planes, drain, 0)
    finish(planes - 1)

    halo[hops] = values[:, :LANES]
    grad_x = values[:, LANES : 2 * LANES]
    grad_y = values[:, 2 * LANES :]

    def halo_copy(number, h):
        return pltpu.make_async_remote_copy(
            src_ref=halo.at[hops], dst_ref=halo.at[hops - h],
            send_sem=halo_send.at[number], recv_sem=halo_recv.at[number],
            device_id=(me, (slab + h + slabs) % slabs), device_id_type=MESH,
        )

    copies = [halo_copy(number, h) for number, h in enumerate(offsets)]
    for copy in copies:
        copy.start()
    for copy in copies:
        copy.wait()
    around = jnp.concatenate([halo[n] for n in range(2 * hops + 1)], axis=1)
    grad_z = split_dot(around, depth_ref[...])
    components = (grad_x, grad_y, grad_z)
    quadratic = jnp.zeros_like(grad_x)
    for i in range(3):
        for j in range(3):
            quadratic = quadratic + metric_ref[i : i + 1, j : j + 1] * components[i] * components[j]
    term = jnp.dot(occ_ref[...], quadratic, precision=HIGHEST, preferred_element_type=jnp.float32)
    terms[me] = jnp.broadcast_to(term, (8, LANES))

    def term_copy(k):
        return pltpu.make_async_remote_copy(
            src_ref=terms.at[me], dst_ref=terms.at[me],
            send_sem=term_send.at[k - 1], recv_sem=term_recv.at[k - 1],
            device_id=((me + k) % bands, slab), device_id_type=MESH,
        )

    for k in range(1, bands):
        term_copy(k).start()

    def sent(p, carry):
        core_copy(p).wait_send()
        for t in range(chips - 1):
            @pl.when((chip < chips - 1 - t) & ((chip > 0) | (p == planes - 1)))
            def _():
                line_copy(0, p, t, line.at[0, p, t], ahead).wait_send()

            @pl.when((chip > t) & ((chip < chips - 1) | (p == planes - 1)))
            def _():
                line_copy(1, p, t, line.at[1, p, t], behind).wait_send()
        return carry

    lax.fori_loop(0, planes, sent, 0)
    for k in range(1, bands):
        term_copy(k).wait()
    summed = terms[0]
    for b in range(1, bands):
        summed = summed + terms[b]
    summed = summed * (0.5 / window)
    for p in range(planes):
        dens_ref[p : p + 1, :] = summed[0:1, p * points : (p + 1) * points]


def local(orbitals, rotation, occupation, metric):
    bands, slabs = lax.axis_size("band"), lax.axis_size("slab")
    orbital_count, planes, plane_size = orbitals.shape
    window = rotation.shape[1]
    owned = window // bands
    chips = bands // 2
    hops = -(-REACH // planes)
    f32 = jnp.float32
    vmem = pl.BlockSpec(memory_space=pltpu.VMEM)
    hbm = pl.BlockSpec(memory_space=pltpu.HBM)
    dma = pltpu.SemaphoreType.DMA
    neighbours = 2 * hops
    rotated, density = pl.pallas_call(
        functools.partial(kernel, (bands, slabs, planes, owned, hops, window)),
        out_shape=(
            jax.ShapeDtypeStruct((planes, owned, plane_size), f32),
            jax.ShapeDtypeStruct((planes, PY * PX), f32),
        ),
        in_specs=[hbm] * 6,
        out_specs=(vmem, vmem),
        scratch_shapes=[
            pltpu.VMEM((1, owned), f32),
            pltpu.VMEM((3, 3), f32),
            pltpu.VMEM((2 * plane_size, 3 * LANES), jnp.bfloat16),
            pltpu.VMEM((2 * (neighbours + 1) * LANES, LANES), jnp.bfloat16),
            pltpu.VMEM((owned, 3 * LANES), f32),
            dma((4,)),
            pltpu.VMEM((planes, orbital_count, plane_size), f32),
            pltpu.VMEM((orbital_count, window), f32),
            pltpu.VMEM((2 * window, orbital_count), jnp.bfloat16),
            pltpu.VMEM((planes, 2, window // 2, plane_size), f32),
            pltpu.VMEM((planes, window // 2, plane_size), f32),
            pltpu.VMEM((planes, window // 2, plane_size), f32),
            pltpu.VMEM((2, planes, chips - 1, owned, plane_size), f32),
            pltpu.VMEM((neighbours + 1, owned, LANES), f32),
            pltpu.VMEM((bands, 8, LANES), f32),
            dma((planes,)),
            dma,
            dma((planes,)),
            dma((planes,)),
            dma((2, planes, chips - 1)),
            dma((2, planes, chips - 1)),
            dma((neighbours,)),
            dma((neighbours,)),
            dma((bands - 1,)),
            dma((bands - 1,)),
        ],
        compiler_params=pltpu.CompilerParams(
            collective_id=0, has_side_effects=True, vmem_limit_bytes=62 * 1024 * 1024
        ),
    )(
        jnp.transpose(orbitals, (1, 0, 2)),
        rotation,
        occupation.reshape(1, owned),
        metric,
        halves(plane_tables()),
        halves(depth_tables(planes, hops).reshape(-1, LANES)),
    )
    return jnp.transpose(rotated, (1, 0, 2)), density


def solution(mesh):
    placed = (P("band", "slab", None), P("band", None), P("band"), P())
    return jax.shard_map(
        local,
        mesh=mesh,
        in_specs=placed,
        out_specs=(P("band", "slab", None), P("slab", None)),
        check_vma=False,
    )
```

```python
import functools

import jax
import jax.numpy as jnp
import ml_dtypes
import numpy as np
from jax import lax
from jax.experimental import pallas as pl
from jax.experimental.pallas import tpu as pltpu
from jax.sharding import PartitionSpec as P

PY = 4
PX = 4
LANES = 128
REACH = 6
WINDOW = 2
MESH = pl.DeviceIdType.MESH
STENCIL_WEIGHTS = (6.0 / 7.0, -15.0 / 56.0, 5.0 / 63.0, -1.0 / 56.0, 6.0 / 1925.0, -1.0 / 5544.0)
HIGHEST = lax.Precision.HIGHEST


def plane_tables():
    stored_x = PX + 12
    table = np.zeros(((PY + 12) * stored_x, 3 * LANES), np.float32)
    for row_y in range(PY):
        for row_x in range(PX):
            point = row_y * PX + row_x
            centre = (row_y + 6) * stored_x + row_x + 6
            table[centre, point] = 1.0
            for distance, weight in enumerate(STENCIL_WEIGHTS, start=1):
                table[centre + distance, LANES + point] += weight
                table[centre - distance, LANES + point] -= weight
                table[centre + distance * stored_x, 2 * LANES + point] += weight
                table[centre - distance * stored_x, 2 * LANES + point] -= weight
    return table


def depth_tables(planes, hops):
    points = PY * PX
    table = np.zeros((2 * hops + 1, LANES, LANES), np.float32)
    for plane in range(planes):
        for distance, weight in enumerate(STENCIL_WEIGHTS, start=1):
            for signed, value in ((distance, weight), (-distance, -weight)):
                slab, source = divmod(plane + signed, planes)
                for point in range(points):
                    table[slab + hops, source * points + point, plane * points + point] += value
    return table


def split_dot(x, table):
    depth = x.shape[1]
    high = x.astype(jnp.bfloat16)
    low = (x - high.astype(jnp.float32)).astype(jnp.bfloat16)
    f32 = jnp.float32
    main = jnp.dot(high, table[:depth], preferred_element_type=f32)
    rest = jnp.dot(low, table[:depth], preferred_element_type=f32)
    return main + (rest + jnp.dot(high, table[depth:], preferred_element_type=f32))


def halves(table):
    high = table.astype(ml_dtypes.bfloat16)
    low = (table - high.astype(np.float32)).astype(ml_dtypes.bfloat16)
    return jnp.asarray(np.concatenate([high, low], axis=0))


def kernel(
    sizes, orb_hbm, rot_hbm, occ_hbm, metric_hbm, plane_hbm, depth_hbm, out_ref, dens_ref,
    occ_ref, metric_ref, plane_ref, depth_ref, values, small_sem, orb, rot, left, part, crecv, sbuf, line, halo, terms,
    orb_sem, rot_sem, core_send, core_recv, line_send, line_recv, halo_send, halo_recv, term_send, term_recv,
):
    bands, slabs, planes, owned, hops, window = sizes
    chips = bands // 2
    me, slab = lax.axis_index("band"), lax.axis_index("slab")
    chip, core = me // 2, me % 2
    points = PY * PX
    partner = (chip * 2 + 1 - core, slab)
    ahead, behind = (me + 2, slab), (me - 2, slab)

    def load(p):
        return pltpu.make_async_copy(orb_hbm.at[p], orb.at[p], orb_sem.at[p])

    load_rot = pltpu.make_async_copy(rot_hbm, rot, rot_sem)
    load_rot.start()
    for p in range(planes):
        load(p).start()
    small_loads = [
        pltpu.make_async_copy(src, dst, small_sem.at[n])
        for n, (src, dst) in enumerate(
            ((occ_hbm, occ_ref), (metric_hbm, metric_ref), (plane_hbm, plane_ref), (depth_hbm, depth_ref))
        )
    ]
    for small_load in small_loads:
        small_load.start()

    barrier = pltpu.get_barrier_semaphore()
    for k in range(1, bands):
        pl.semaphore_signal(barrier, inc=1, device_id=((me + k) % bands, slab), device_id_type=MESH)
    offsets = [h for h in range(-hops, hops + 1) if h != 0]
    for h in offsets:
        pl.semaphore_signal(barrier, inc=1, device_id=(me, (slab + h + slabs) % slabs), device_id_type=MESH)

    load_rot.wait()
    for chip_at in range(chips):
        rows = jnp.transpose(rot[:, chip_at * 2 * owned : (chip_at + 1) * 2 * owned])
        high = rows.astype(jnp.bfloat16)
        low = (rows - high.astype(jnp.float32)).astype(jnp.bfloat16)
        for core_at in range(2):
            at = (core_at * chips + chip_at) * owned
            left[at : at + owned, :] = high[core_at * owned : (core_at + 1) * owned]
            left[window + at : window + at + owned, :] = low[core_at * owned : (core_at + 1) * owned]

    def core_copy(p):
        return pltpu.make_async_remote_copy(
            src_ref=part.at[p, 1 - core], dst_ref=crecv.at[p], send_sem=core_send.at[p], recv_sem=core_recv.at[p],
            device_id=partner, device_id_type=MESH,
        )

    def multiply(p):
        load(p).wait()
        field = orb[p]
        high = field.astype(jnp.bfloat16)
        low = (field - high.astype(jnp.float32)).astype(jnp.bfloat16)
        both = jnp.dot(left[...], high, preferred_element_type=jnp.float32)
        small = jnp.dot(left[:window, :], low, preferred_element_type=jnp.float32)
        total = both[:window] + (both[window:] + small)
        part[p] = total.reshape(2, window // 2, total.shape[-1])

    def line_copy(direction, p, t, src, target):
        return pltpu.make_async_remote_copy(
            src_ref=src, dst_ref=line.at[direction, p, t],
            send_sem=line_send.at[direction, p, t], recv_sem=line_recv.at[direction, p, t],
            device_id=target, device_id_type=MESH,
        )

    def block(d):
        return pl.ds(pl.multiple_of(d * owned, owned), owned)

    def originate(p):
        core_copy(p).wait_recv()
        sbuf[p] = part[p, core] + crecv[p]
        for t in range(chips - 1):
            @pl.when(chip == 0)
            def _():
                @pl.when(p >= WINDOW)
                def _():
                    line_copy(0, p - WINDOW, t, sbuf.at[p - WINDOW, block(chips - 1 - t)], ahead).wait_send()

                line_copy(0, p, t, sbuf.at[p, block(chips - 1 - t)], ahead).start()

            @pl.when(chip == chips - 1)
            def _():
                @pl.when(p >= WINDOW)
                def _():
                    line_copy(1, p - WINDOW, t, sbuf.at[p - WINDOW, block(t)], behind).wait_send()

                line_copy(1, p, t, sbuf.at[p, block(t)], behind).start()
        out_ref[p] = sbuf[p, block(chip), :]

    def transit(p, near):
        def rightward(t):
            @pl.when((chip > 0) & (chip < chips - 1 - t))
            def _():
                line_copy(0, p, t, line.at[0, p, t], behind).wait_recv()
                line[0, p, t] += sbuf[p, block(chips - 1 - t), :]
                line_copy(0, p, t, line.at[0, p, t], ahead).start()

        def leftward(t):
            @pl.when((chip < chips - 1) & (chip > t))
            def _():
                line_copy(1, p, t, line.at[1, p, t], ahead).wait_recv()
                line[1, p, t] += sbuf[p, block(t), :]
                line_copy(1, p, t, line.at[1, p, t], behind).start()

        @pl.when((chip < chips // 2) if near else (chip >= chips // 2))
        def _():
            for t in range(chips - 1):
                rightward(t)

        @pl.when((chip >= chips // 2) if near else (chip < chips // 2))
        def _():
            for t in range(chips - 1):
                leftward(t)

    def finish(p):
        @pl.when(chip > 0)
        def _():
            t = chips - 1 - chip
            line_copy(0, p, t, line.at[0, p, t], behind).wait_recv()
            out_ref[p] += line[0, p, t]

        @pl.when(chip < chips - 1)
        def _():
            line_copy(1, p, chip, line.at[1, p, chip], ahead).wait_recv()
            out_ref[p] += line[1, p, chip]

        found = split_dot(out_ref[p], plane_ref[...])
        for g in range(3):
            group = found[:, g * LANES : (g + 1) * LANES]
            values[:, g * LANES : (g + 1) * LANES] += pltpu.roll(group, p * points, 1)

    multiply(0)
    pl.semaphore_wait(barrier, bands - 1 + len(offsets))
    core_copy(0).start()
    values[...] = jnp.zeros_like(values)
    for small_load in small_loads:
        small_load.wait()

    def step(p, carry):
        multiply(p)
        core_copy(p).start()
        originate(p - 1)

        @pl.when(p >= 2)
        def _():
            transit(p - 2, True)

        @pl.when(p >= 3)
        def _():
            transit(p - 3, False)

        return carry

    lax.fori_loop(1, planes, step, 0)
    originate(planes - 1)

    def early(p, carry):
        finish(p)
        return carry

    def late(p, carry):
        transit(p, True)
        @pl.when(p >= 1)
        def _():
            transit(p - 1, False)

        @pl.when(p >= 2)
        def _():
            finish(p - 2)

        return carry

    lax.fori_loop(0, max(planes - 4, 0), early, 0)
    lax.fori_loop(planes - 2, planes, late, 0)
    transit(planes - 1, False)
    finish(planes - 2)
    finish(planes - 1)

    halo[hops] = values[:, :LANES]
    grad_x = values[:, LANES : 2 * LANES]
    grad_y = values[:, 2 * LANES :]

    def halo_copy(number, h):
        return pltpu.make_async_remote_copy(
            src_ref=halo.at[hops], dst_ref=halo.at[hops - h],
            send_sem=halo_send.at[number], recv_sem=halo_recv.at[number],
            device_id=(me, (slab + h + slabs) % slabs), device_id_type=MESH,
        )

    copies = [halo_copy(number, h) for number, h in enumerate(offsets)]
    for copy in copies:
        copy.start()
    for copy in copies:
        copy.wait()
    around = jnp.concatenate([halo[n] for n in range(2 * hops + 1)], axis=1)
    grad_z = split_dot(around, depth_ref[...])
    components = (grad_x, grad_y, grad_z)
    quadratic = jnp.zeros_like(grad_x)
    for i in range(3):
        for j in range(3):
            quadratic = quadratic + metric_ref[i : i + 1, j : j + 1] * components[i] * components[j]
    term = jnp.dot(occ_ref[...], quadratic, precision=HIGHEST, preferred_element_type=jnp.float32)
    terms[me] = jnp.broadcast_to(term, (8, LANES))

    def term_copy(k):
        return pltpu.make_async_remote_copy(
            src_ref=terms.at[me], dst_ref=terms.at[me],
            send_sem=term_send.at[k - 1], recv_sem=term_recv.at[k - 1],
            device_id=((me + k) % bands, slab), device_id_type=MESH,
        )

    for k in range(1, bands):
        term_copy(k).start()

    def sent(p, carry):
        core_copy(p).wait_send()
        for t in range(chips - 1):
            @pl.when((chip < chips - 1 - t) & ((chip > 0) | (p >= planes - WINDOW)))
            def _():
                line_copy(0, p, t, line.at[0, p, t], ahead).wait_send()

            @pl.when((chip > t) & ((chip < chips - 1) | (p >= planes - WINDOW)))
            def _():
                line_copy(1, p, t, line.at[1, p, t], behind).wait_send()
        return carry

    lax.fori_loop(0, planes, sent, 0)
    for k in range(1, bands):
        term_copy(k).wait()
    summed = terms[0]
    for b in range(1, bands):
        summed = summed + terms[b]
    summed = summed * (0.5 / window)
    for p in range(planes):
        dens_ref[p : p + 1, :] = summed[0:1, p * points : (p + 1) * points]


def local(orbitals, rotation, occupation, metric):
    bands, slabs = lax.axis_size("band"), lax.axis_size("slab")
    orbital_count, planes, plane_size = orbitals.shape
    window = rotation.shape[1]
    owned = window // bands
    chips = bands // 2
    hops = -(-REACH // planes)
    f32 = jnp.float32
    vmem = pl.BlockSpec(memory_space=pltpu.VMEM)
    hbm = pl.BlockSpec(memory_space=pltpu.HBM)
    dma = pltpu.SemaphoreType.DMA
    neighbours = 2 * hops
    rotated, density = pl.pallas_call(
        functools.partial(kernel, (bands, slabs, planes, owned, hops, window)),
        out_shape=(
            jax.ShapeDtypeStruct((planes, owned, plane_size), f32),
            jax.ShapeDtypeStruct((planes, PY * PX), f32),
        ),
        in_specs=[hbm] * 6,
        out_specs=(vmem, vmem),
        scratch_shapes=[
            pltpu.VMEM((1, owned), f32),
            pltpu.VMEM((3, 3), f32),
            pltpu.VMEM((2 * plane_size, 3 * LANES), jnp.bfloat16),
            pltpu.VMEM((2 * (neighbours + 1) * LANES, LANES), jnp.bfloat16),
            pltpu.VMEM((owned, 3 * LANES), f32),
            dma((4,)),
            pltpu.VMEM((planes, orbital_count, plane_size), f32),
            pltpu.VMEM((orbital_count, window), f32),
            pltpu.VMEM((2 * window, orbital_count), jnp.bfloat16),
            pltpu.VMEM((planes, 2, window // 2, plane_size), f32),
            pltpu.VMEM((planes, window // 2, plane_size), f32),
            pltpu.VMEM((planes, window // 2, plane_size), f32),
            pltpu.VMEM((2, planes, chips - 1, owned, plane_size), f32),
            pltpu.VMEM((neighbours + 1, owned, LANES), f32),
            pltpu.VMEM((bands, 8, LANES), f32),
            dma((planes,)),
            dma,
            dma((planes,)),
            dma((planes,)),
            dma((2, planes, chips - 1)),
            dma((2, planes, chips - 1)),
            dma((neighbours,)),
            dma((neighbours,)),
            dma((bands - 1,)),
            dma((bands - 1,)),
        ],
        compiler_params=pltpu.CompilerParams(
            collective_id=0, has_side_effects=True, vmem_limit_bytes=62 * 1024 * 1024
        ),
    )(
        jnp.transpose(orbitals, (1, 0, 2)),
        rotation,
        occupation.reshape(1, owned),
        metric,
        halves(plane_tables()),
        halves(depth_tables(planes, hops).reshape(-1, LANES)),
    )
    return jnp.transpose(rotated, (1, 0, 2)), density


def solution(mesh):
    placed = (P("band", "slab", None), P("band", None), P("band"), P())
    return jax.shard_map(
        local,
        mesh=mesh,
        in_specs=placed,
        out_specs=(P("band", "slab", None), P("slab", None)),
        check_vma=False,
    )
```

```python
import functools

import jax
import jax.numpy as jnp
import ml_dtypes
import numpy as np
from jax import lax
from jax.experimental import pallas as pl
from jax.experimental.pallas import tpu as pltpu
from jax.sharding import PartitionSpec as P

PY = 4
PX = 4
LANES = 128
REACH = 6
WINDOW = 2
MESH = pl.DeviceIdType.MESH
STENCIL_WEIGHTS = (6.0 / 7.0, -15.0 / 56.0, 5.0 / 63.0, -1.0 / 56.0, 6.0 / 1925.0, -1.0 / 5544.0)
HIGHEST = lax.Precision.HIGHEST


def plane_tables():
    stored_x = PX + 12
    table = np.zeros(((PY + 12) * stored_x, 3 * LANES), np.float32)
    for row_y in range(PY):
        for row_x in range(PX):
            point = row_y * PX + row_x
            centre = (row_y + 6) * stored_x + row_x + 6
            table[centre, point] = 1.0
            for distance, weight in enumerate(STENCIL_WEIGHTS, start=1):
                table[centre + distance, LANES + point] += weight
                table[centre - distance, LANES + point] -= weight
                table[centre + distance * stored_x, 2 * LANES + point] += weight
                table[centre - distance * stored_x, 2 * LANES + point] -= weight
    return table


def depth_tables(planes, hops):
    points = PY * PX
    table = np.zeros((2 * hops + 1, LANES, LANES), np.float32)
    for plane in range(planes):
        for distance, weight in enumerate(STENCIL_WEIGHTS, start=1):
            for signed, value in ((distance, weight), (-distance, -weight)):
                slab, source = divmod(plane + signed, planes)
                for point in range(points):
                    table[slab + hops, source * points + point, plane * points + point] += value
    return table


def split_dot(x, table):
    depth = x.shape[1]
    high = x.astype(jnp.bfloat16)
    low = (x - high.astype(jnp.float32)).astype(jnp.bfloat16)
    f32 = jnp.float32
    main = jnp.dot(high, table[:depth], preferred_element_type=f32)
    rest = jnp.dot(low, table[:depth], preferred_element_type=f32)
    return main + (rest + jnp.dot(high, table[depth:], preferred_element_type=f32))


def halves(table):
    high = table.astype(ml_dtypes.bfloat16)
    low = (table - high.astype(np.float32)).astype(ml_dtypes.bfloat16)
    return jnp.asarray(np.concatenate([high, low], axis=0))


def kernel(
    sizes, orb_hbm, rot_hbm, occ_hbm, metric_hbm, plane_hbm, depth_hbm, out_ref, dens_ref,
    occ_ref, metric_ref, plane_ref, depth_ref, values, small_sem, orb, rot, left, part, crecv, sbuf, line, halo, terms,
    orb_sem, rot_sem, core_send, core_recv, line_send, line_recv, halo_send, halo_recv, term_send, term_recv,
):
    bands, slabs, planes, owned, hops, window = sizes
    chips = bands // 2
    me, slab = lax.axis_index("band"), lax.axis_index("slab")
    chip, core = me // 2, me % 2
    points = PY * PX
    partner = (chip * 2 + 1 - core, slab)
    ahead, behind = (me + 2, slab), (me - 2, slab)

    def load(p):
        return pltpu.make_async_copy(orb_hbm.at[p], orb.at[p], orb_sem.at[p])

    load_rot = pltpu.make_async_copy(rot_hbm, rot, rot_sem)
    load_rot.start()
    for p in range(planes):
        load(p).start()
    small_loads = [
        pltpu.make_async_copy(src, dst, small_sem.at[n])
        for n, (src, dst) in enumerate(
            ((occ_hbm, occ_ref), (metric_hbm, metric_ref), (plane_hbm, plane_ref), (depth_hbm, depth_ref))
        )
    ]
    for small_load in small_loads:
        small_load.start()

    barrier = pltpu.get_barrier_semaphore()
    for k in range(1, bands):
        pl.semaphore_signal(barrier, inc=1, device_id=((me + k) % bands, slab), device_id_type=MESH)
    offsets = [h for h in range(-hops, hops + 1) if h != 0]
    for h in offsets:
        pl.semaphore_signal(barrier, inc=1, device_id=(me, (slab + h + slabs) % slabs), device_id_type=MESH)

    load_rot.wait()
    for chip_at in range(chips):
        rows = jnp.transpose(rot[:, chip_at * 2 * owned : (chip_at + 1) * 2 * owned])
        high = rows.astype(jnp.bfloat16)
        low = (rows - high.astype(jnp.float32)).astype(jnp.bfloat16)
        for core_at in range(2):
            at = (core_at * chips + chip_at) * owned
            left[at : at + owned, :] = high[core_at * owned : (core_at + 1) * owned]
            left[window + at : window + at + owned, :] = low[core_at * owned : (core_at + 1) * owned]

    def core_copy(p):
        return pltpu.make_async_remote_copy(
            src_ref=part.at[p, 1 - core], dst_ref=crecv.at[p], send_sem=core_send.at[p], recv_sem=core_recv.at[p],
            device_id=partner, device_id_type=MESH,
        )

    def multiply(p):
        load(p).wait()
        field = orb[p]
        high = field.astype(jnp.bfloat16)
        low = (field - high.astype(jnp.float32)).astype(jnp.bfloat16)
        both = jnp.dot(left[...], high, preferred_element_type=jnp.float32)
        small = jnp.dot(left[:window, :], low, preferred_element_type=jnp.float32)
        total = both[:window] + (both[window:] + small)
        part[p] = total.reshape(2, window // 2, total.shape[-1])

    def line_copy(direction, p, t, src, target):
        return pltpu.make_async_remote_copy(
            src_ref=src, dst_ref=line.at[direction, p, t],
            send_sem=line_send.at[direction, p, t], recv_sem=line_recv.at[direction, p, t],
            device_id=target, device_id_type=MESH,
        )

    def block(d):
        return pl.ds(pl.multiple_of(d * owned, owned), owned)

    def originate(p):
        core_copy(p).wait_recv()
        sbuf[p] = part[p, core] + crecv[p]
        for t in range(chips - 1):
            @pl.when(chip == 0)
            def _():
                @pl.when(p >= WINDOW)
                def _():
                    line_copy(0, p - WINDOW, t, sbuf.at[p - WINDOW, block(chips - 1 - t)], ahead).wait_send()

                line_copy(0, p, t, sbuf.at[p, block(chips - 1 - t)], ahead).start()

            @pl.when(chip == chips - 1)
            def _():
                @pl.when(p >= WINDOW)
                def _():
                    line_copy(1, p - WINDOW, t, sbuf.at[p - WINDOW, block(t)], behind).wait_send()

                line_copy(1, p, t, sbuf.at[p, block(t)], behind).start()
        out_ref[p] = sbuf[p, block(chip), :]

    def transit(p, near):
        def rightward(t):
            @pl.when((chip > 0) & (chip < chips - 1 - t))
            def _():
                line_copy(0, p, t, line.at[0, p, t], behind).wait_recv()
                line[0, p, t] += sbuf[p, block(chips - 1 - t), :]
                line_copy(0, p, t, line.at[0, p, t], ahead).start()

        def leftward(t):
            @pl.when((chip < chips - 1) & (chip > t))
            def _():
                line_copy(1, p, t, line.at[1, p, t], ahead).wait_recv()
                line[1, p, t] += sbuf[p, block(t), :]
                line_copy(1, p, t, line.at[1, p, t], behind).start()

        @pl.when((chip < chips // 2) if near else (chip >= chips // 2))
        def _():
            for t in range(chips - 1):
                rightward(t)

        @pl.when((chip >= chips // 2) if near else (chip < chips // 2))
        def _():
            for t in range(chips - 1):
                leftward(t)

    def finish(p):
        @pl.when(chip > 0)
        def _():
            t = chips - 1 - chip
            line_copy(0, p, t, line.at[0, p, t], behind).wait_recv()
            out_ref[p] += line[0, p, t]

        @pl.when(chip < chips - 1)
        def _():
            line_copy(1, p, chip, line.at[1, p, chip], ahead).wait_recv()
            out_ref[p] += line[1, p, chip]

        found = split_dot(out_ref[p], plane_ref[...])
        for g in range(3):
            group = found[:, g * LANES : (g + 1) * LANES]
            values[:, g * LANES : (g + 1) * LANES] += pltpu.roll(group, p * points, 1)

    multiply(0)
    pl.semaphore_wait(barrier, bands - 1 + len(offsets))
    core_copy(0).start()
    values[...] = jnp.zeros_like(values)
    for small_load in small_loads:
        small_load.wait()

    def step(p, carry):
        multiply(p)
        core_copy(p).start()
        originate(p - 1)

        @pl.when(p >= 3)
        def _():
            transit(p - 3, True)

        @pl.when(p >= 4)
        def _():
            transit(p - 4, False)

        return carry

    lax.fori_loop(1, planes, step, 0)
    originate(planes - 1)

    def early(p, carry):
        finish(p)
        return carry

    def late(p, carry):
        transit(p, True)
        @pl.when(p >= 1)
        def _():
            transit(p - 1, False)

        @pl.when(p >= 2)
        def _():
            finish(p - 2)

        return carry

    lax.fori_loop(0, max(planes - 5, 0), early, 0)
    lax.fori_loop(planes - 3, planes, late, 0)
    transit(planes - 1, False)
    finish(planes - 2)
    finish(planes - 1)

    halo[hops] = values[:, :LANES]
    grad_x = values[:, LANES : 2 * LANES]
    grad_y = values[:, 2 * LANES :]

    def halo_copy(number, h):
        return pltpu.make_async_remote_copy(
            src_ref=halo.at[hops], dst_ref=halo.at[hops - h],
            send_sem=halo_send.at[number], recv_sem=halo_recv.at[number],
            device_id=(me, (slab + h + slabs) % slabs), device_id_type=MESH,
        )

    copies = [halo_copy(number, h) for number, h in enumerate(offsets)]
    for copy in copies:
        copy.start()
    for copy in copies:
        copy.wait()
    around = jnp.concatenate([halo[n] for n in range(2 * hops + 1)], axis=1)
    grad_z = split_dot(around, depth_ref[...])
    components = (grad_x, grad_y, grad_z)
    quadratic = jnp.zeros_like(grad_x)
    for i in range(3):
        for j in range(3):
            quadratic = quadratic + metric_ref[i : i + 1, j : j + 1] * components[i] * components[j]
    term = jnp.dot(occ_ref[...], quadratic, precision=HIGHEST, preferred_element_type=jnp.float32)
    terms[me] = jnp.broadcast_to(term, (8, LANES))

    def term_copy(k):
        return pltpu.make_async_remote_copy(
            src_ref=terms.at[me], dst_ref=terms.at[me],
            send_sem=term_send.at[k - 1], recv_sem=term_recv.at[k - 1],
            device_id=((me + k) % bands, slab), device_id_type=MESH,
        )

    for k in range(1, bands):
        term_copy(k).start()

    def sent(p, carry):
        core_copy(p).wait_send()
        for t in range(chips - 1):
            @pl.when((chip < chips - 1 - t) & ((chip > 0) | (p >= planes - WINDOW)))
            def _():
                line_copy(0, p, t, line.at[0, p, t], ahead).wait_send()

            @pl.when((chip > t) & ((chip < chips - 1) | (p >= planes - WINDOW)))
            def _():
                line_copy(1, p, t, line.at[1, p, t], behind).wait_send()
        return carry

    lax.fori_loop(0, planes, sent, 0)
    for k in range(1, bands):
        term_copy(k).wait()
    summed = terms[0]
    for b in range(1, bands):
        summed = summed + terms[b]
    summed = summed * (0.5 / window)
    for p in range(planes):
        dens_ref[p : p + 1, :] = summed[0:1, p * points : (p + 1) * points]


def local(orbitals, rotation, occupation, metric):
    bands, slabs = lax.axis_size("band"), lax.axis_size("slab")
    orbital_count, planes, plane_size = orbitals.shape
    window = rotation.shape[1]
    owned = window // bands
    chips = bands // 2
    hops = -(-REACH // planes)
    f32 = jnp.float32
    vmem = pl.BlockSpec(memory_space=pltpu.VMEM)
    hbm = pl.BlockSpec(memory_space=pltpu.HBM)
    dma = pltpu.SemaphoreType.DMA
    neighbours = 2 * hops
    rotated, density = pl.pallas_call(
        functools.partial(kernel, (bands, slabs, planes, owned, hops, window)),
        out_shape=(
            jax.ShapeDtypeStruct((planes, owned, plane_size), f32),
            jax.ShapeDtypeStruct((planes, PY * PX), f32),
        ),
        in_specs=[hbm] * 6,
        out_specs=(vmem, vmem),
        scratch_shapes=[
            pltpu.VMEM((1, owned), f32),
            pltpu.VMEM((3, 3), f32),
            pltpu.VMEM((2 * plane_size, 3 * LANES), jnp.bfloat16),
            pltpu.VMEM((2 * (neighbours + 1) * LANES, LANES), jnp.bfloat16),
            pltpu.VMEM((owned, 3 * LANES), f32),
            dma((4,)),
            pltpu.VMEM((planes, orbital_count, plane_size), f32),
            pltpu.VMEM((orbital_count, window), f32),
            pltpu.VMEM((2 * window, orbital_count), jnp.bfloat16),
            pltpu.VMEM((planes, 2, window // 2, plane_size), f32),
            pltpu.VMEM((planes, window // 2, plane_size), f32),
            pltpu.VMEM((planes, window // 2, plane_size), f32),
            pltpu.VMEM((2, planes, chips - 1, owned, plane_size), f32),
            pltpu.VMEM((neighbours + 1, owned, LANES), f32),
            pltpu.VMEM((bands, 8, LANES), f32),
            dma((planes,)),
            dma,
            dma((planes,)),
            dma((planes,)),
            dma((2, planes, chips - 1)),
            dma((2, planes, chips - 1)),
            dma((neighbours,)),
            dma((neighbours,)),
            dma((bands - 1,)),
            dma((bands - 1,)),
        ],
        compiler_params=pltpu.CompilerParams(
            collective_id=0, has_side_effects=True, vmem_limit_bytes=62 * 1024 * 1024
        ),
    )(
        jnp.transpose(orbitals, (1, 0, 2)),
        rotation,
        occupation.reshape(1, owned),
        metric,
        halves(plane_tables()),
        halves(depth_tables(planes, hops).reshape(-1, LANES)),
    )
    return jnp.transpose(rotated, (1, 0, 2)), density


def solution(mesh):
    placed = (P("band", "slab", None), P("band", None), P("band"), P())
    return jax.shard_map(
        local,
        mesh=mesh,
        in_specs=placed,
        out_specs=(P("band", "slab", None), P("slab", None)),
        check_vma=False,
    )
```
